32 devices in a mesh: seg: 4 (over z), seq: 8 (over y, x, core).
Axes of the slice: x: 2, y: 2, z: 4, core: 2. Of those that a mesh axis runs over, the one named last changes fastest.
Arguments:
- keyframe_latents: bfloat16 [4, 1024, 1536], P('seg', 'seq'), may hold values from -24 to 24
- keyframe_steps: int32 [4], P('seg'), may hold values from 0 to 63
- infill_latents: bfloat16 [4, 2, 1024, 1536], P('seg', None, 'seq'), may hold values from -24 to 24
- infill_steps: int32 [4, 2], P('seg'), may hold values from 0 to 63
- bounds: int32 [4, 2], P('seg'), may hold values from 0 to 3, as said below
- shift_table: float32 [64, 1536], replicated, may hold values from -4 to 4
- scale_table: float32 [64, 1536], replicated, may hold values from -0.5 to 1.5
- gate_table: float32 [64, 1536], replicated, may hold values from 0.5 to 2.5
- query_weight: bfloat16 [1536, 2048], P(None, 'seq'), may hold values from -0.15625 to 0.15625
- key_weight: bfloat16 [1536, 2048], P(None, 'seq'), may hold values from -0.15625 to 0.15625
- value_weight: bfloat16 [1536, 2048], P(None, 'seq'), may hold values from -0.15625 to 0.15625
- out_weight: bfloat16 [2048, 1536], P('seq'), may hold values from -0.125 to 0.125
- query_gain: float32 [128], replicated, may hold values from 0.5 to 2
- key_gain: float32 [128], replicated, may hold values from 0.5 to 2
Outputs:
- keyframe_out: bfloat16 [4, 1024, 1536], P('seg', 'seq')
- infill_out: bfloat16 [4, 2, 1024, 1536], P('seg', None, 'seq')
The draws below stay inside these ranges and needn't reach their ends.
Inputs may be any that keep to these rules, and one draw needn't show every extreme that they name: `bounds`: the two keyframes of a segment differ.
All inputs are finite; a program needn't handle non-finite values.
Results may differ from the reference program's by a relative error of at most 0.0052.
Values may be sent and summed in bfloat16 or wider, within the bound.
No kernel may reach another device: no remote copies, remote signals or barrier semaphores. Data moves between devices by JAX's collectives and lax.ppermute only.
A program may use at most 192 MiB of HBM per device.

```python
import math
import jax
import jax.numpy as jnp
from jax import lax

D = 1536
HEADS = 16
HEAD = 128
STEPS = 64
FRAMES = 2
HD = 2048
FRAME_TOK = 1024
KEYS = 4
SEGS = 4


def latent_field(key, leading):
    key_feat, key_rows, key_base = jax.random.split(key, 3)
    features = jnp.exp(jax.random.uniform(key_feat, (D,), jnp.float32, math.log(0.3), math.log(3.0)))
    row_scales = jnp.exp(jax.random.uniform(key_rows, leading + (FRAME_TOK, 1), jnp.float32, math.log(0.5), math.log(2.0)))
    base = jax.random.normal(key_base, leading + (FRAME_TOK, D), jnp.float32)
    base = jnp.clip(base, -4.0, 4.0)
    return (base * features * row_scales).astype(jnp.bfloat16)


def draw_keyframe_latents(key, part):
    return latent_field(jax.random.fold_in(key, 11), (KEYS,))


def draw_infill_latents(key, part):
    return latent_field(jax.random.fold_in(key, 23), (SEGS, FRAMES))


def draw_bounds(key, part):
    key_left, key_step = jax.random.split(jax.random.fold_in(key, 37))
    left_one = jax.random.randint(key_left, (SEGS,), 0, KEYS, dtype=jnp.int32)
    stride = jax.random.randint(key_step, (SEGS,), 1, KEYS, dtype=jnp.int32)
    right_one = (left_one + stride) % KEYS
    return jnp.stack([left_one, right_one], axis=1).astype(jnp.int32)


def with_ends(entries, stream_key, smallest, top_value):
    spot = [jax.random.randint(jax.random.fold_in(stream_key, axis), (), 0, length) for axis, length in enumerate(entries.shape)]
    widest = entries.shape.index(max(entries.shape))
    neighbour = spot[:widest] + [(spot[widest] + 1) % entries.shape[widest]] + spot[widest + 1:]
    return entries.at[tuple(spot)].set(smallest).at[tuple(neighbour)].set(top_value)


def steps_of(rng, dims, cuts, least, largest):
    level, own = 1.0, jax.random.fold_in(rng, 6)
    for axis_at, parts in cuts:
        steps = jnp.exp(jax.random.uniform(jax.random.fold_in(own, axis_at), (parts,), jnp.float32, least / len(cuts), largest / len(cuts)))
        level = level * jnp.repeat(steps, dims[axis_at] // parts).reshape([-1 if axis == axis_at else 1 for axis in range(len(dims))])
    return level


def centred(key, extent, deviation, reach, cuts=(), kind=jnp.bfloat16):
    entries = deviation * jax.random.normal(key, extent, jnp.float32)
    if cuts:
        entries = entries * steps_of(key, extent, cuts, -0.22, 0.18)
    return jnp.clip(entries, -reach, reach).astype(kind)


def setup_inputs(seed: int = 0) -> dict:
    keys = jax.random.split(jax.random.key(seed), 15)
    return {
        "keyframe_latents": draw_keyframe_latents(jax.random.fold_in(keys[14], 71), 0),
        "keyframe_steps": with_ends(jax.random.randint(keys[1], (KEYS,), 0, STEPS), jax.random.fold_in(keys[1], 1), 0, STEPS - 1).astype(jnp.int32),
        "infill_latents": draw_infill_latents(jax.random.fold_in(keys[14], 71), 0),
        "infill_steps": with_ends(jax.random.randint(keys[3], (SEGS, FRAMES), 0, STEPS), jax.random.fold_in(keys[3], 1), 0, STEPS - 1).astype(jnp.int32),
        "bounds": draw_bounds(jax.random.fold_in(keys[14], 71), 0),
        "shift_table": centred(keys[5], (STEPS, D), 1.0, 4.0, (), jnp.float32),
        "scale_table": jnp.clip(jax.random.uniform(keys[6], (STEPS, D), jnp.float32, -0.5, 1.5), -0.5, 1.5),
        "gate_table": jnp.clip(jax.random.uniform(keys[7], (STEPS, D), jnp.float32, 0.5, 2.5), 0.5, 2.5),
        "query_weight": centred(keys[8], (D, HD), D ** -0.5, 0.15625, ((1, 8),)),
        "key_weight": centred(keys[9], (D, HD), D ** -0.5, 0.15625, ((1, 8),)),
        "value_weight": centred(keys[10], (D, HD), D ** -0.5, 0.15625, ((1, 8),)),
        "out_weight": centred(keys[11], (HD, D), HD ** -0.5, 0.125, ((0, 8),)),
        "query_gain": jnp.clip(jnp.exp(jax.random.uniform(keys[12], (HEAD,), jnp.float32, math.log(0.5), math.log(2.0))), 0.5, 2.0),
        "key_gain": jnp.clip(jnp.exp(jax.random.uniform(keys[13], (HEAD,), jnp.float32, math.log(0.5), math.log(2.0))), 0.5, 2.0),
    }


EPSILON = 1e-06

def lookup(steps, table):
    onehot = (steps[:, None] == jnp.arange(STEPS, dtype=jnp.int32)[None, :]).astype(jnp.float32)
    return jnp.dot(onehot, table, precision=lax.Precision.HIGHEST)

def modulate(latents, steps, shift_table, scale_table):
    shifts = lookup(steps, shift_table)
    scales = lookup(steps, scale_table)
    values = latents.astype(jnp.float32)
    center = values - lax.optimization_barrier(jnp.mean(values, axis=-1, keepdims=True))
    normed = center * lax.rsqrt(lax.optimization_barrier(jnp.mean(center * center, axis=-1, keepdims=True)) + EPSILON)
    return (normed * (1.0 + scales[:, None, :]) + shifts[:, None, :]).astype(jnp.bfloat16)

def head_norm(projected, gain):
    flat_rows = projected.shape[0]
    shaped = projected.reshape(flat_rows, HEADS, HEAD)
    normed = shaped * lax.rsqrt(lax.optimization_barrier(jnp.mean(shaped * shaped, axis=-1, keepdims=True)) + EPSILON) * gain
    return normed.reshape(flat_rows, HEADS * HEAD).astype(jnp.bfloat16)

def project(modded, query_weight, key_weight, value_weight, query_gain, key_gain):
    flat = modded.reshape(-1, D)
    query_rows = head_norm(jnp.dot(flat, query_weight, preferred_element_type=jnp.float32), query_gain)
    key_rows = head_norm(jnp.dot(flat, key_weight, preferred_element_type=jnp.float32), key_gain)
    value_rows = jnp.dot(flat, value_weight, preferred_element_type=jnp.float32).astype(jnp.bfloat16)
    shape = (modded.shape[0], FRAME_TOK, HEADS * HEAD)
    return (query_rows.reshape(shape), key_rows.reshape(shape), value_rows.reshape(shape))

def attend_head(query_rows, key_rows, value_rows):
    scores = jnp.dot(query_rows, key_rows.T, preferred_element_type=jnp.float32) * (1.0 / math.sqrt(HEAD))
    powers = jnp.exp(scores)
    weights = (powers / lax.optimization_barrier(jnp.sum(powers, axis=1, keepdims=True))).astype(jnp.bfloat16)
    return jnp.dot(weights, value_rows, preferred_element_type=jnp.float32).astype(jnp.bfloat16)

def split_heads(rows):
    return rows.reshape(rows.shape[0], HEADS, HEAD).transpose(1, 0, 2)

def attend_frame(query_rows, key_rows, value_rows):
    result = lax.map(lambda triple: attend_head(triple[0], triple[1], triple[2]), (split_heads(query_rows), split_heads(key_rows), split_heads(value_rows)))
    return result.transpose(1, 0, 2).reshape(query_rows.shape[0], HEADS * HEAD)

def finish(latents, steps, attention, out_weight, gate_table):
    gates = lookup(steps, gate_table)
    branch = jnp.dot(attention.reshape(-1, HEADS * HEAD), out_weight, preferred_element_type=jnp.float32)
    branch = branch.reshape(latents.shape)
    return (latents.astype(jnp.float32) + gates[:, None, :] * branch).astype(jnp.bfloat16)

def reference(keyframe_latents, keyframe_steps, infill_latents, infill_steps, bounds, shift_table, scale_table, gate_table, query_weight, key_weight, value_weight, out_weight, query_gain, key_gain):
    key_mod = modulate(keyframe_latents, keyframe_steps, shift_table, scale_table)
    key_query, key_keys, key_values = project(key_mod, query_weight, key_weight, value_weight, query_gain, key_gain)
    key_att = lax.map(lambda triple: attend_frame(triple[0], triple[1], triple[2]), (key_query, key_keys, key_values))
    keyframe_out = finish(keyframe_latents, keyframe_steps, key_att, out_weight, gate_table)
    flat_latents = infill_latents.reshape(SEGS * FRAMES, FRAME_TOK, D)
    flat_steps = infill_steps.reshape(SEGS * FRAMES)
    infill_mod = modulate(flat_latents, flat_steps, shift_table, scale_table)
    infill_query, infill_keys, infill_values = project(infill_mod, query_weight, key_weight, value_weight, query_gain, key_gain)
    owners = (jnp.arange(SEGS * FRAMES, dtype=jnp.int32) // FRAMES).astype(jnp.int32)
    left_index = bounds[owners, 0].astype(jnp.int32)
    right_index = bounds[owners, 1].astype(jnp.int32)

    def infill_frame(bundle):
        query_rows, own_keys, own_values, left_one, right_one = bundle
        key_rows = jnp.concatenate([own_keys, key_keys[left_one], key_keys[right_one]], axis=0)
        value_rows = jnp.concatenate([own_values, key_values[left_one], key_values[right_one]], axis=0)
        return attend_frame(query_rows, key_rows, value_rows)
    infill_att = lax.map(infill_frame, (infill_query, infill_keys, infill_values, left_index, right_index))
    infill_out = finish(flat_latents, flat_steps, infill_att, out_weight, gate_table)
    return (keyframe_out, infill_out.reshape(infill_latents.shape))
```

```python
import functools
import math

import jax
import jax.numpy as jnp
from jax import lax
from jax.experimental import pallas as pl
from jax.experimental.pallas import tpu as pltpu
from jax.sharding import PartitionSpec as P

HEAD = 128
EPSILON = 1e-06
ANY = pl.BlockSpec(memory_space=pl.ANY)


def swap(value, mask, count):
    return lax.ppermute(value, "seq", [(i, i ^ mask) for i in range(count)])


def modulate_kernel(steps_ref, latents_ref, shift_ref, scale_ref, out_ref):
    row = lax.rem(steps_ref[pl.program_id(0)], 8)
    values = latents_ref[0].astype(jnp.float32)
    center = values - jnp.mean(values, axis=-1, keepdims=True)
    normed = center * lax.rsqrt(jnp.mean(center * center, axis=-1, keepdims=True) + EPSILON)
    scales = scale_ref[pl.ds(row, 1), :]
    shifts = shift_ref[pl.ds(row, 1), :]
    out_ref[0] = (normed * (1.0 + scales) + shifts).astype(jnp.bfloat16)


def modulate(latents, steps, shift_table, scale_table):
    frames, tokens, width = latents.shape
    frame_spec = pl.BlockSpec((1, tokens, width), lambda f, s: (f, 0, 0))
    table_spec = pl.BlockSpec((8, width), lambda f, s: (s[f] // 8, 0))
    return pl.pallas_call(
        modulate_kernel,
        out_shape=jax.ShapeDtypeStruct(latents.shape, jnp.bfloat16),
        grid_spec=pltpu.PrefetchScalarGridSpec(
            num_scalar_prefetch=1,
            grid=(frames,),
            in_specs=[frame_spec, table_spec, table_spec],
            out_specs=frame_spec,
        ),
        cost_estimate=pl.CostEstimate(
            flops=10 * latents.size, bytes_accessed=4 * latents.size, transcendentals=0
        ),
        compiler_params=pltpu.CompilerParams(vmem_limit_bytes=16 << 20),
        name="modulate",
    )(steps, latents, shift_table, scale_table)


def gather_chips(chunk, count):
    axis = chunk.ndim - 2
    rows = chunk.shape[axis]
    bits = [1 << b for b in range(1, count.bit_length() - 1)]
    if len(bits) == 2:
        half = rows // 2
        over_x = swap(chunk, bits[0], count)
        over_y = swap(chunk, bits[1], count)
        far_low = swap(lax.slice_in_dim(over_x, 0, half, axis=axis), bits[1], count)
        far_high = swap(lax.slice_in_dim(over_y, half, rows, axis=axis), bits[0], count)
        return [chunk, over_x, over_y, far_low, far_high]
    pieces = [chunk]
    for bit in bits:
        pieces += [swap(piece, bit, count) for piece in pieces]
    return pieces


def project_kernel(
    piece_count, weight_count, *refs
):
    pieces = refs[:piece_count]
    weights = refs[piece_count : piece_count + 2 * weight_count]
    gain_refs = refs[piece_count + 2 * weight_count : piece_count + 2 * weight_count + 2]
    out_refs = refs[piece_count + 2 * weight_count + 2 : piece_count + 2 * weight_count + 4]
    flat, held, piece_sems, weight_sems = refs[piece_count + 2 * weight_count + 4 :]
    frames, total = flat.shape[0], flat.shape[1]
    copies = []
    for frame in range(frames):
        offset = 0
        for index, piece in enumerate(pieces):
            rows = piece.shape[1]
            copies.append(
                pltpu.make_async_copy(
                    piece.at[frame],
                    flat.at[frame, pl.ds(offset, rows)],
                    piece_sems.at[frame, index],
                )
            )
            offset += rows
    for copy in copies:
        copy.start()
    loads = [
        pltpu.make_async_copy(weight, held.at[index], weight_sems.at[index])
        for index, weight in enumerate(weights)
    ]
    for load in loads:
        load.start()
    for copy in copies:
        copy.wait()
    width = held.shape[2]
    heads = width // HEAD
    tile = math.gcd(256, total)
    for index in range(2 * weight_count):
        loads[index].wait()
        side, kind = divmod(index, weight_count)
        place = kind * width
        gain_ref = None if kind == weight_count - 1 else gain_refs[kind + 3 - weight_count]
        for frame in range(frames):

            def body(step, carry, index=index, place=place, gain_ref=gain_ref, frame=frame, side=side):
                start = pl.multiple_of(step * tile, tile)
                result = jnp.dot(
                    flat[frame, pl.ds(start, tile), :],
                    held[index],
                    preferred_element_type=jnp.float32,
                )
                for head in range(heads):
                    part = result[:, head * HEAD : (head + 1) * HEAD]
                    if gain_ref is not None:
                        mean = jnp.mean(part * part, axis=-1, keepdims=True)
                        part = part * lax.rsqrt(mean + EPSILON) * gain_ref[...]
                    out_refs[side][
                        frame, pl.ds(start, tile), place + head * HEAD : place + (head + 1) * HEAD
                    ] = part.astype(jnp.bfloat16)
                return carry

            lax.fori_loop(0, total // tile, body, 0)


def project(pieces, weights, gains):
    frames, _, depth = pieces[0].shape
    total = sum(piece.shape[1] for piece in pieces)
    width = weights[0].shape[1]
    weight_count = len(weights) // 2
    out = jax.ShapeDtypeStruct((frames, total, weight_count * width), jnp.bfloat16)
    vmem = pl.BlockSpec(memory_space=pltpu.VMEM)
    flops = 2 * frames * total * depth * width * len(weights)
    return pl.pallas_call(
        functools.partial(project_kernel, len(pieces), weight_count),
        out_shape=(out, out),
        in_specs=[ANY] * (len(pieces) + len(weights)) + [vmem, vmem],
        out_specs=(vmem, vmem),
        scratch_shapes=[
            pltpu.VMEM((frames, total, depth), jnp.bfloat16),
            pltpu.VMEM((len(weights), depth, width), jnp.bfloat16),
            pltpu.SemaphoreType.DMA((frames, len(pieces))),
            pltpu.SemaphoreType.DMA((len(weights),)),
        ],
        cost_estimate=pl.CostEstimate(
            flops=flops, bytes_accessed=2 * len(weights) * depth * width, transcendentals=0
        ),
        compiler_params=pltpu.CompilerParams(vmem_limit_bytes=32 << 20),
        name="project",
    )(*pieces, *weights, *gains)


def attend_kernel(width, first, last, token_rows, me_ref, *refs):
    query_refs, key_refs, value_refs = refs[0:2], refs[2:4], refs[4:6]
    out_ref = refs[-1]
    sum_ref = None if first else refs[6]
    heads = width // HEAD
    rows = query_refs[0].shape[1]
    key_rows = key_refs[0].shape[1]
    tile = math.gcd(256, rows)
    chunk = math.gcd(512, key_rows)
    ones = jnp.ones((chunk, HEAD), jnp.bfloat16)
    for head in range(heads):
        lanes = slice(head * HEAD, (head + 1) * HEAD)
        wide = slice(head * 2 * HEAD, (head + 1) * 2 * HEAD)
        for side in range(2):
            for start in range(0, rows, tile):
                queries = query_refs[side][0, start : start + tile, lanes]
                place = side * rows + start
                total = None if first else sum_ref[0, place : place + tile, wide]
                for other in range(2):
                    for base in range(0, key_rows, chunk):
                        keys = key_refs[other][0, base : base + chunk, lanes]
                        values = value_refs[other][0, base : base + chunk, lanes]
                        scores = lax.dot_general(
                            queries,
                            keys,
                            (((1,), (1,)), ((), ())),
                            preferred_element_type=jnp.float32,
                        )
                        powers = jnp.exp2(scores).astype(jnp.bfloat16)
                        part = jnp.dot(
                            powers,
                            jnp.concatenate([values, ones], axis=1),
                            preferred_element_type=jnp.float32,
                        )
                        total = part if total is None else total + part
                if last:
                    result = (total[:, :HEAD] / total[:, HEAD:]).astype(jnp.bfloat16)
                    for block in range(0, tile, token_rows):
                        piece = (start + block) // token_rows
                        target = me_ref[0] ^ (2 * piece + side)
                        out_ref[target, 0, :, lanes] = result[block : block + token_rows]
                else:
                    out_ref[0, place : place + tile, wide] = total


def attend(me, queries, keys, sums, width, last, token_rows, key_frame):
    frames, rows, _ = queries[0].shape
    columns = keys[0].shape[2] // width
    key_rows = keys[0].shape[1]
    first = sums is None
    count = 2 * rows // token_rows

    def pick(column, follows):
        if follows:
            return lambda f, me: (f, 0, column)
        return lambda f, me: (key_frame, 0, column)

    follows = key_frame is None
    in_specs = (
        [pl.BlockSpec((1, rows, width), pick(0, True))] * 2
        + [pl.BlockSpec((1, key_rows, width), pick(columns - 2, follows))] * 2
        + [pl.BlockSpec((1, key_rows, width), pick(columns - 1, follows))] * 2
    )
    args = [*queries, *keys, *keys]
    sum_spec = pl.BlockSpec((1, 2 * rows, 2 * width), lambda f, me: (f, 0, 0))
    if not first:
        in_specs.append(sum_spec)
        args.append(sums)
    if last:
        out = jax.ShapeDtypeStruct((count, frames, token_rows, width), jnp.bfloat16)
        out_spec = pl.BlockSpec((count, 1, token_rows, width), lambda f, me: (0, f, 0, 0))
    else:
        out = jax.ShapeDtypeStruct((frames, 2 * rows, 2 * width), jnp.float32)
        out_spec = sum_spec
    work = frames * 2 * rows * 2 * key_rows * width
    return pl.pallas_call(
        functools.partial(attend_kernel, width, first, last, token_rows),
        out_shape=out,
        grid_spec=pltpu.PrefetchScalarGridSpec(
            num_scalar_prefetch=1, grid=(frames,), in_specs=in_specs, out_specs=out_spec
        ),
        cost_estimate=pl.CostEstimate(
            flops=8 * work, bytes_accessed=8 * frames * rows * width, transcendentals=work // HEAD
        ),
        compiler_params=pltpu.CompilerParams(vmem_limit_bytes=32 << 20),
        name="attend",
    )(me, *args)


def finish(scalars, heads, latents, gate_table, pieces):
    frames, tokens, width = latents.shape
    count, _, _, depth = heads.shape
    vmem = pl.BlockSpec(memory_space=pltpu.VMEM)
    smem = pl.BlockSpec(memory_space=pltpu.SMEM)
    flat = heads.reshape(count, frames * tokens, depth)
    columns = math.gcd(512, width)
    sides = len(pieces) // 2

    def kernel(scalars_ref, heads_ref, latents_ref, gate_ref, *refs):
        weight_refs = refs[: len(pieces)]
        out_ref, held, sems = refs[len(pieces) :]
        loads = []
        for side in range(2):
            offset = 0
            for index in range(sides):
                piece = weight_refs[side * sides + index]
                rows = piece.shape[0]
                loads.append(
                    pltpu.make_async_copy(
                        piece, held.at[side, pl.ds(offset, rows)], sems.at[side * sides + index]
                    )
                )
                offset += rows
        for load in loads:
            load.start()
        for load in loads:
            load.wait()
        me = scalars_ref[0]
        for column in range(0, width, columns):
            lanes = slice(column, column + columns)
            total = None
            for side in range(2):
                for index in range(count // 2):
                    part = jnp.dot(
                        heads_ref[me ^ (2 * index + side)],
                        held[side, index * depth : (index + 1) * depth, lanes],
                        preferred_element_type=jnp.float32,
                    )
                    total = part if total is None else total + part
            for frame in range(frames):
                gate = gate_ref[pl.ds(scalars_ref[1 + frame], 1), lanes]
                branch = total[frame * tokens : (frame + 1) * tokens]
                base = latents_ref[frame, :, lanes].astype(jnp.float32)
                out_ref[frame, :, lanes] = (base + gate * branch).astype(jnp.bfloat16)

    return pl.pallas_call(
        kernel,
        out_shape=jax.ShapeDtypeStruct(latents.shape, jnp.bfloat16),
        in_specs=[smem, vmem, vmem, vmem] + [ANY] * len(pieces),
        out_specs=vmem,
        scratch_shapes=[
            pltpu.VMEM((2, count // 2 * depth, width), jnp.bfloat16),
            pltpu.SemaphoreType.DMA((len(pieces),)),
        ],
        cost_estimate=pl.CostEstimate(
            flops=2 * frames * tokens * count * depth * width,
            bytes_accessed=2 * count * depth * width,
            transcendentals=0,
        ),
        compiler_params=pltpu.CompilerParams(vmem_limit_bytes=32 << 20),
        name="finish",
    )(scalars, flat, latents, gate_table, *pieces)


def local(
    segs,
    count,
    keyframe_latents,
    keyframe_steps,
    infill_latents,
    infill_steps,
    bounds,
    shift_table,
    scale_table,
    gate_table,
    query_weight,
    key_weight,
    value_weight,
    out_weight,
    query_gain,
    key_gain,
):
    width = query_weight.shape[1]
    frames, tokens, features = infill_latents.shape[1:]
    infill = infill_latents.reshape(frames, tokens, features)
    infill_at = infill_steps.reshape(frames)
    me = lax.axis_index("seq").astype(jnp.int32).reshape(1)
    seg = lax.axis_index("seg").astype(jnp.int32)

    key_mod = modulate(keyframe_latents, keyframe_steps, shift_table, scale_table)
    key_slots = [key_mod] + [
        lax.ppermute(key_mod, "seg", [(i, (i + d) % segs) for i in range(segs)])
        for d in range(1, segs)
    ]
    infill_mod = modulate(infill, infill_at, shift_table, scale_table)
    infill_pieces = gather_chips(infill_mod, count)
    key_pieces = gather_chips(key_mod, count)

    own = [query_weight, key_weight, value_weight]
    theirs = [swap(weight, 1, count) for weight in own]
    scale = math.log2(math.e) / math.sqrt(HEAD)
    gains = [(query_gain * scale).reshape(1, HEAD), key_gain.reshape(1, HEAD)]

    def heads_of(pieces, with_query):
        kinds = slice(0, 3) if with_query else slice(1, 3)
        mine, other = project(pieces, own[kinds] + theirs[kinds], gains)
        return [mine, swap(other, 1, count)]

    infill_heads = heads_of(infill_pieces, True)
    sums = attend(me, infill_heads, infill_heads, None, width, False, tokens, None)

    key_heads = heads_of(key_pieces, True)
    key_att = attend(me, key_heads, key_heads, None, width, True, tokens, None)
    key_back = lax.all_to_all(key_att, "seq", split_axis=0, concat_axis=0, tiled=True)

    for side in range(2):
        slot = lax.rem(seg - bounds[0, side] + segs, segs)
        chosen = lax.select_n(slot, *key_slots)
        cond_heads = heads_of(gather_chips(chosen, count), False)
        sums = attend(me, infill_heads, cond_heads, sums, width, side == 1, tokens, 0)
    infill_back = lax.all_to_all(sums, "seq", split_axis=0, concat_axis=0, tiled=True)

    weight_pieces = gather_chips(out_weight, count)
    weight_pieces = weight_pieces + [swap(piece, 1, count) for piece in weight_pieces]
    keyframe_out = finish(
        jnp.concatenate([me, keyframe_steps]), key_back, keyframe_latents, gate_table, weight_pieces
    )
    infill_out = finish(
        jnp.concatenate([me, infill_at]), infill_back, infill, gate_table, weight_pieces
    )
    return (keyframe_out, infill_out.reshape(infill_latents.shape))


def solution(mesh):
    return jax.shard_map(
        functools.partial(local, mesh.shape["seg"], mesh.shape["seq"]),
        mesh=mesh,
        in_specs=(
            P("seg", "seq", None),
            P("seg"),
            P("seg", None, "seq", None),
            P("seg", None),
            P("seg", None),
            P(),
            P(),
            P(),
            P(None, "seq"),
            P(None, "seq"),
            P(None, "seq"),
            P("seq", None),
            P(),
            P(),
        ),
        out_specs=(P("seg", "seq", None), P("seg", None, "seq", None)),
        check_vma=False,
    )
```
